256 devices in a mesh: seq: 64 (over z, y, core), head: 4 (over x).
Axes of the slice: x: 4, y: 4, z: 8, core: 2. Of those that a mesh axis runs over, the one named last changes fastest.
Arguments:
- queries: bfloat16 [16384, 8192], P('seq', 'head'), may hold values from -6 to 6
- keys: bfloat16 [16384, 8192], P('seq', 'head'), may hold values from -6 to 6
- values: bfloat16 [16384, 8192], P('seq', 'head'), may hold values from -20 to 20
- out_grad: bfloat16 [16384, 8192], P('seq', 'head'), may hold values from -6 to 6
- norm_gain: bfloat16 [8192], P('head'), may hold values from 0.099609375 to 1.8984375
Outputs:
- query_grad: bfloat16 [16384, 8192], P('seq', 'head')
- key_grad: bfloat16 [16384, 8192], P('seq', 'head')
- value_grad: bfloat16 [16384, 8192], P('seq', 'head')
The draws below stay inside these ranges and needn't reach their ends.
All inputs are finite; a program needn't handle non-finite values.
Results may differ from the reference program's by a relative error of at most 0.0058.
Values sent between devices are 32-bit elements; how exact they have to be, the bound alone decides.
A program may use at most 192 MiB of HBM per device.

```python
import jax
import jax.numpy as jnp
from jax import lax

HEADS = 64
DH = 128
GROUP = 256
SEQ = 16384


def draw_values(key, part):
    width = HEADS * DH
    head_of = jnp.arange(width) // DH
    rising = 3.0 ** (0.5 * head_of.astype(jnp.float32) / (HEADS - 1))
    sample = jnp.clip(jax.random.normal(jax.random.fold_in(key, 4), (SEQ, width), jnp.float32), -4.0, 4.0)
    result = sample * rising[None, :]
    return result.astype(jnp.bfloat16)


def levels(key, dims, cuts, smallest, largest):
    loudness = 1.0
    for position, blocks in cuts:
        steps = jax.random.uniform(jax.random.fold_in(jax.random.fold_in(key, 6), position), (blocks,), jnp.float32, smallest / len(cuts), largest / len(cuts))
        loudness = loudness * jnp.repeat(jnp.exp(steps), dims[position] // blocks).reshape((-1,) + (1,) * (len(dims) - 1 - position))
    return loudness


def normal_values(key, shape, scale, reach, shards=(), held_as=jnp.bfloat16):
    values = jax.random.normal(key, shape, jnp.float32) * scale
    if len(shards) > 0:
        values = levels(key, shape, shards, -0.22, 0.18) * values
    return jnp.clip(values, min=-reach, max=reach).astype(held_as)


def setup_inputs(seed: int = 0) -> dict:
    streams_of = jax.random.split(jax.random.key(seed), 6)
    return {
        "queries": normal_values(streams_of[0], (SEQ, HEADS * DH), 1.0, 6.0, ((0, 64), (1, 4))),
        "keys": normal_values(streams_of[1], (SEQ, HEADS * DH), 1.0, 6.0, ((0, 64), (1, 4))),
        "values": draw_values(jax.random.fold_in(streams_of[5], 71), 0),
        "out_grad": normal_values(streams_of[3], (SEQ, HEADS * DH), 1.0, 6.0, ((0, 64), (1, 4))),
        "norm_gain": jnp.clip(1.0 + 0.18 * jax.random.normal(streams_of[4], (HEADS * DH,), jnp.float32), 0.099609375, 1.8984375).astype(jnp.bfloat16),
    }


def round_bf(array):
    return lax.optimization_barrier(array.astype(jnp.bfloat16)).astype(jnp.float32)

def causal_mask(count):
    rows = lax.broadcasted_iota(jnp.int32, (count, count), 0)
    cols = lax.broadcasted_iota(jnp.int32, (count, count), 1)
    return (rows >= cols).astype(jnp.float32)

def reference(queries, keys, values, out_grad, norm_gain):
    blocks = SEQ // GROUP
    features = HEADS * DH
    highest = lax.Precision.HIGHEST
    masking = causal_mask(GROUP)
    gain = norm_gain.astype(jnp.float32)

    def split(array):
        return array.reshape(blocks, GROUP, HEADS, DH)
    query_b, key_b, value_b = (split(queries), split(keys), split(values))
    grad_rows = out_grad.reshape(blocks, GROUP, features)

    def forward(state, inputs):
        query_c, key_c, value_c, grad_c = inputs
        query_f = query_c.astype(jnp.float32)
        key_f = key_c.astype(jnp.float32)
        value_f = value_c.astype(jnp.float32)
        state_b = round_bf(state)
        scores = jnp.einsum('chd,khd->hck', query_f, key_f, precision=highest)
        masked = round_bf(scores * masking[None])
        attn = jnp.einsum('hck,khd->chd', masked, value_f, precision=highest)
        attn = attn + jnp.einsum('chd,hde->che', query_f, state_b, precision=highest)
        attn = attn.reshape(GROUP, features)
        scaled = gain[None, :] * grad_c.astype(jnp.float32)
        inverse = lax.rsqrt(lax.optimization_barrier(jnp.sum(attn * attn, axis=1, keepdims=True)) / features + 1e-05)
        cross = lax.optimization_barrier(jnp.sum(scaled * attn, axis=1, keepdims=True)) / features
        delta = (inverse * scaled - attn * inverse * inverse * inverse * cross).astype(jnp.bfloat16)
        delta_f = delta.astype(jnp.float32).reshape(GROUP, HEADS, DH)
        dscore = round_bf(jnp.einsum('che,khe->hck', delta_f, value_f, precision=highest) * masking[None])
        query_grad = jnp.einsum('hck,khd->chd', dscore, key_f, precision=highest)
        query_grad = query_grad + jnp.einsum('che,hde->chd', delta_f, state_b, precision=highest)
        new_state = state + jnp.einsum('chd,che->hde', key_f, value_f, precision=highest)
        return (new_state, (query_grad.astype(jnp.bfloat16), delta.reshape(GROUP, HEADS, DH)))
    start = jnp.zeros((HEADS, DH, DH), jnp.float32)
    unused, (query_grad, deltas) = lax.scan(forward, start, (query_b, key_b, value_b, grad_rows))

    def backward(later, inputs):
        query_c, key_c, value_c, delta_c = inputs
        query_f = query_c.astype(jnp.float32)
        key_f = key_c.astype(jnp.float32)
        value_f = value_c.astype(jnp.float32)
        delta_f = delta_c.astype(jnp.float32)
        later_b = round_bf(later)
        scores = jnp.einsum('chd,khd->hck', query_f, key_f, precision=highest)
        masked = round_bf(scores * masking[None])
        dscore = round_bf(jnp.einsum('che,khe->hck', delta_f, value_f, precision=highest) * masking[None])
        key_grad = jnp.einsum('hck,chd->khd', dscore, query_f, precision=highest)
        key_grad = key_grad + jnp.einsum('che,hde->chd', value_f, later_b, precision=highest)
        value_grad = jnp.einsum('hck,che->khe', masked, delta_f, precision=highest)
        value_grad = value_grad + jnp.einsum('chd,hde->che', key_f, later_b, precision=highest)
        new_later = later + jnp.einsum('chd,che->hde', query_f, delta_f, precision=highest)
        return (new_later, (key_grad.astype(jnp.bfloat16), value_grad.astype(jnp.bfloat16)))
    unused_two, (key_grad, value_grad) = lax.scan(backward, start, (query_b, key_b, value_b, deltas), reverse=True)
    return (query_grad.reshape(SEQ, features), key_grad.reshape(SEQ, features), value_grad.reshape(SEQ, features))
```

```python
import jax
import jax.numpy as jnp
from jax import lax
from jax.experimental import pallas as pl
from jax.experimental.pallas import tpu as pltpu
from jax.sharding import PartitionSpec as P

DH = 128
GROUP = 256
HEADS = 16
HALF = 8
NZ = 8
NY = 4
CHIPS = NZ * NY
NX = 4
ROWS = HALF * DH // CHIPS
SPLIT = DH // ROWS
MESH = pl.DeviceIdType.MESH
FAR_Z = (4, 3, 5, 2, 6, 1, 7, 0)
FAR_Y = (2, 1, 3, 0)
OFFSETS = [(dz, dy) for dz in FAR_Z for dy in FAR_Y if (dz, dy) != (0, 0)]

f32 = jnp.float32
bf16 = jnp.bfloat16


def dot(a, b, dim_a, dim_b):
    return lax.dot_general(
        a, b, (((dim_a,), (dim_b,)), ((), ())), preferred_element_type=f32
    )


def kernel(
    q_hbm, k_hbm, v_hbm, g_hbm, gain_ref,
    qg_hbm, kg_hbm, vg_hbm,
    q, k, v, g, attn, delta, scores, dscore, qg, kg, vg, state,
    own, swap, chip, gather, parts, back, ahead, arrived,
    norm_send, norm_got,
    in_sem, out_sem, swap_sem, out_a2a_sem, back_send_sem, back_sem, ahead_sem, norm_sem,
):
    seq = lax.axis_index("seq")
    plane = lax.axis_index("head")
    core = lax.rem(seq, 2)
    here = seq // 2
    z, y = here // NY, lax.rem(here, NY)
    other = (seq + 1 - 2 * core, plane)

    def chip_at(dz, dy):
        return lax.rem(z + dz, NZ) * NY + lax.rem(y + dy, NY)

    def device_of(place):
        return (place * 2 + core, plane)

    def across(step):
        return (seq, lax.rem(plane + step, NX))

    loads = [
        pltpu.make_async_copy(src, dst, in_sem.at[i])
        for i, (src, dst) in enumerate(((k_hbm, k), (v_hbm, v), (q_hbm, q), (g_hbm, g)))
    ]
    for load in loads:
        load.start()

    barrier = pltpu.get_barrier_semaphore()
    pl.semaphore_signal(barrier, inc=1, device_id=other, device_id_type=MESH)
    for dz, dy in OFFSETS:
        pl.semaphore_signal(
            barrier, inc=1, device_id=device_of(chip_at(dz, dy)), device_id_type=MESH
        )
    for step in range(1, NX):
        pl.semaphore_signal(barrier, inc=1, device_id=across(step), device_id_type=MESH)

    mine = core * HALF
    theirs = HALF - mine

    def cols(head):
        return pl.ds(pl.multiple_of(head * DH, DH), DH)

    def each(first, body):
        def one(i, carry):
            body(i, first + i)
            return carry

        lax.fori_loop(0, HALF, one, 0)

    def swap_half(s, term, first):
        def fill(half):
            def body(i, head):
                own[s, half, pl.ds(i * SPLIT, SPLIT)] = term(head).reshape(SPLIT, ROWS, DH)

            return body

        each(theirs, fill(1 - core))
        if first:
            pl.semaphore_wait(barrier, 1 + len(OFFSETS) + NX - 1)
        copy = pltpu.make_async_remote_copy(
            src_ref=own.at[s, 1 - core],
            dst_ref=swap.at[s],
            send_sem=swap_sem.at[s, 0],
            recv_sem=swap_sem.at[s, 1],
            device_id=other,
            device_id_type=MESH,
        )
        copy.start()
        each(mine, fill(core))
        copy.wait()
        chip[s] = own[s, core] + swap[s]

    def spread(s):
        for dz, dy in OFFSETS:
            place = chip_at(dz, dy)
            pltpu.make_async_remote_copy(
                src_ref=chip.at[s, place],
                dst_ref=gather.at[s, here],
                send_sem=out_a2a_sem.at[s, 0],
                recv_sem=out_a2a_sem.at[s, 1],
                device_id=device_of(place),
                device_id_type=MESH,
            ).start()
        gather[s, here] = chip[s, here]

    def wait_for(ref, sem):
        pltpu.make_async_copy(ref, ref, sem).wait()

    def sum_up(s, reverse):
        wait_for(gather.at[s, pl.ds(0, CHIPS - 1)], out_a2a_sem.at[s, 1])
        total = jnp.zeros((ROWS, DH), f32)
        for place in range(CHIPS - 1, -1, -1) if reverse else range(CHIPS):
            parts[s, place] = total
            total = total + gather[s, place]

    def send_back(s):
        for dz, dy in OFFSETS:
            place = chip_at(dz, dy)
            pltpu.make_async_remote_copy(
                src_ref=parts.at[s, place],
                dst_ref=back.at[s, here],
                send_sem=back_send_sem.at[s],
                recv_sem=back_sem.at[s, here // SPLIT],
                device_id=device_of(place),
                device_id_type=MESH,
            ).start()
        pltpu.make_async_copy(
            parts.at[s, here], back.at[s, here], back_sem.at[s, here // SPLIT]
        ).start()

    def ahead_copy(s, i):
        return pltpu.make_async_remote_copy(
            src_ref=ahead.at[s, i],
            dst_ref=arrived.at[s, i],
            send_sem=ahead_sem.at[s, 0, i],
            recv_sem=ahead_sem.at[s, 1, i],
            device_id=other,
            device_id_type=MESH,
        )

    def collect(s, inner, use):
        def mine_one(i, head):
            rows = pl.ds(i * SPLIT, SPLIT)
            wait_for(back.at[s, rows], back_sem.at[s, i])
            chip_part = back[s, rows].reshape(DH, DH)
            here_is_inner = core == inner
            extra = jnp.where(here_is_inner, own[s, core, rows], swap[s, rows]).reshape(DH, DH)
            both = chip_part + extra
            ahead[s, i] = jnp.where(here_is_inner, both, chip_part)
            ahead_copy(s, i).start()
            use(head, jnp.where(here_is_inner, chip_part, both).astype(bf16))

        each(mine, mine_one)

        def theirs_one(i, head):
            ahead_copy(s, i).wait_recv()
            use(head, arrived[s, i].astype(bf16))

        each(theirs, theirs_one)

    def finish_sends(s):
        sent = pl.ds(0, CHIPS - 1)
        wait_for(chip.at[s, sent], out_a2a_sem.at[s, 0])
        wait_for(parts.at[s, sent], back_send_sem.at[s])
        each(0, lambda i, head: ahead_copy(s, i).wait_send())

    rows = lax.broadcasted_iota(jnp.int32, (GROUP, GROUP), 0)
    columns = lax.broadcasted_iota(jnp.int32, (GROUP, GROUP), 1)
    causal = rows >= columns

    loads[0].wait()
    loads[1].wait()
    swap_half(0, lambda head: dot(k[:, cols(head)], v[:, cols(head)], 0, 0), True)
    spread(0)
    loads[2].wait()
    loads[3].wait()

    def within(i, head):
        at = cols(head)
        part = dot(q[:, at], k[:, at], 1, 1)
        masked = jnp.where(causal, part, 0.0).astype(bf16)
        scores[head] = masked
        attn[:, at] = dot(masked, v[:, at], 1, 0)

    each(0, within)
    sum_up(0, False)
    send_back(0)
    each(HALF, within)

    squares = norm_send.at[0]
    crosses = norm_send.at[1]
    squares[...] = jnp.zeros_like(squares)
    crosses[...] = jnp.zeros_like(crosses)

    def finish_attn(head, state_b):
        at = cols(head)
        state[head] = state_b
        value = attn[:, at] + dot(q[:, at], state_b, 1, 0)
        attn[:, at] = value
        squares[...] += value * value
        crosses[...] += gain_ref[:, at].astype(f32) * g[:, at].astype(f32) * value

    collect(0, 0, finish_attn)

    norm_got[plane, 0:1] = jnp.sum(squares[...].T, axis=0, keepdims=True)
    norm_got[plane, 1:2] = jnp.sum(crosses[...].T, axis=0, keepdims=True)
    for step in range(1, NX):
        pltpu.make_async_remote_copy(
            src_ref=norm_got.at[plane],
            dst_ref=norm_got.at[plane],
            send_sem=norm_sem.at[0],
            recv_sem=norm_sem.at[1],
            device_id=across(step),
            device_id_type=MESH,
        ).start()
    wait_for(norm_got.at[pl.ds(0, NX - 1)], norm_sem.at[1])
    sums = norm_got[0] + norm_got[1] + norm_got[2] + norm_got[3]
    features = float(NX * HEADS * DH)
    inverse = lax.rsqrt(sums[0:1] / features + 1e-05)
    weight = inverse * inverse * inverse * (sums[1:2] / features)
    wait_for(norm_got.at[pl.ds(0, NX - 1)], norm_sem.at[0])
    squares[...] = jnp.broadcast_to(inverse, (DH, GROUP)).T
    crosses[...] = jnp.broadcast_to(weight, (DH, GROUP)).T

    def outer(head):
        at = cols(head)
        scaled = gain_ref[:, at].astype(f32) * g[:, at].astype(f32)
        value = (squares[...] * scaled - attn[:, at] * crosses[...]).astype(bf16)
        delta[:, at] = value
        return dot(q[:, at], value, 0, 0)

    swap_half(1, outer, False)
    spread(1)

    def query_side(i, head):
        at = cols(head)
        part = dot(delta[:, at], v[:, at], 1, 1)
        masked = jnp.where(causal, part, 0.0).astype(bf16)
        dscore[head] = masked
        grad = dot(masked, k[:, at], 1, 0) + dot(delta[:, at], state[head], 1, 1)
        qg[:, at] = grad.astype(bf16)

    each(0, query_side)
    each(HALF, query_side)
    qg_out = pltpu.make_async_copy(qg, qg_hbm, out_sem.at[0])
    qg_out.start()
    sum_up(1, True)
    send_back(1)

    def key_side(i, head):
        at = cols(head)
        kg[:, at] = dot(dscore[head], q[:, at], 0, 0)
        vg[:, at] = dot(scores[head], delta[:, at], 0, 0)

    each(0, key_side)
    each(HALF, key_side)

    def finish_keys(head, later_b):
        at = cols(head)
        k_grad = kg[:, at] + dot(v[:, at], later_b, 1, 1)
        v_grad = vg[:, at] + dot(k[:, at], later_b, 1, 0)
        q[:, at] = k_grad.astype(bf16)
        g[:, at] = v_grad.astype(bf16)

    collect(1, 1, finish_keys)
    kg_out = pltpu.make_async_copy(q, kg_hbm, out_sem.at[1])
    vg_out = pltpu.make_async_copy(g, vg_hbm, out_sem.at[2])
    kg_out.start()
    vg_out.start()
    finish_sends(0)
    finish_sends(1)
    qg_out.wait()
    kg_out.wait()
    vg_out.wait()


def shards(queries, keys, values, out_grad, norm_gain):
    tokens, width = queries.shape
    vmem = pltpu.VMEM
    grad = jax.ShapeDtypeStruct((tokens, width), bf16)
    hbm = pl.BlockSpec(memory_space=pl.ANY)
    slices = (2, CHIPS, ROWS, DH)
    halves = (2, 2, CHIPS, ROWS, DH)
    dma = pltpu.SemaphoreType.DMA
    return pl.pallas_call(
        kernel,
        out_shape=(grad, grad, grad),
        in_specs=[hbm, hbm, hbm, hbm, pl.BlockSpec(memory_space=pltpu.VMEM)],
        out_specs=(hbm, hbm, hbm),
        scratch_shapes=[
            vmem((tokens, width), bf16),
            vmem((tokens, width), bf16),
            vmem((tokens, width), bf16),
            vmem((tokens, width), bf16),
            vmem((tokens, width), f32),
            vmem((tokens, width), bf16),
            vmem((HEADS, GROUP, GROUP), bf16),
            vmem((HEADS, GROUP, GROUP), bf16),
            vmem((tokens, width), bf16),
            vmem((tokens, width), f32),
            vmem((tokens, width), f32),
            vmem((HEADS, DH, DH), bf16),
            vmem(halves, f32),
            vmem(slices, f32),
            vmem(slices, f32),
            vmem(slices, f32),
            vmem(slices, f32),
            vmem(slices, f32),
            vmem((2, HALF, DH, DH), f32),
            vmem((2, HALF, DH, DH), f32),
            vmem((2, GROUP, DH), f32),
            vmem((NX, 8, GROUP), f32),
            dma((4,)),
            dma((3,)),
            dma((2, 2)),
            dma((2, 2)),
            dma((2,)),
            dma((2, HALF)),
            dma((2, 2, HALF)),
            dma((2,)),
        ],
        compiler_params=pltpu.CompilerParams(
            collective_id=0, has_side_effects=True, vmem_limit_bytes=56 * 2**20
        ),
        name="block_backward",
    )(queries, keys, values, out_grad, norm_gain.reshape(1, width))


def solution(mesh):
    return jax.shard_map(
        shards,
        mesh=mesh,
        in_specs=(
            P("seq", "head"),
            P("seq", "head"),
            P("seq", "head"),
            P("seq", "head"),
            P("head"),
        ),
        out_specs=(P("seq", "head"), P("seq", "head"), P("seq", "head")),
        check_vma=False,
    )
```

```python
import jax
import jax.numpy as jnp
from jax import lax
from jax.experimental import pallas as pl
from jax.experimental.pallas import tpu as pltpu
from jax.sharding import PartitionSpec as P

DH = 128
GROUP = 256
HEADS = 16
HALF = 8
NZ = 8
NY = 4
NX = 4
CHUNKS = 4
PER = HALF // CHUNKS
YROWS = PER * DH // NY
ZROWS = YROWS // NZ
MESH = pl.DeviceIdType.MESH
FAR_Z = (4, 3, 5, 2, 6, 1, 7)
FAR_Y = (2, 1, 3)
PEERS = 1 + len(FAR_Z) + len(FAR_Y) + NX - 1

f32 = jnp.float32
bf16 = jnp.bfloat16


def dot(a, b, dim_a, dim_b):
    return lax.dot_general(
        a, b, (((dim_a,), (dim_b,)), ((), ())), preferred_element_type=f32
    )


def wait_for(ref, sem):
    pltpu.make_async_copy(ref, ref, sem).wait()


def kernel(
    q_hbm, k_hbm, v_hbm, g_hbm, gain_hbm,
    qg, kg, vg,
    q, k, v, g, gain, q_t, attn, scaled, delta, scores, dscore, kg_part, vg_part, state,
    own, swap, chip, y_got, y_sum, z_got, z_part, z_back, y_part, y_back, ahead, arrived,
    norm_acc, norm_got,
    in_sem, swap_sem, y_sem, z_sem, zb_sem, yb_sem, ahead_sem, norm_sem,
):
    seq = lax.axis_index("seq")
    plane = lax.axis_index("head")
    core = lax.rem(seq, 2)
    z, y = seq // (2 * NY), lax.rem(seq // 2, NY)
    other = (seq + 1 - 2 * core, plane)
    y_peers = [lax.rem(y + step, NY) for step in FAR_Y]
    z_peers = [lax.rem(z + step, NZ) for step in FAR_Z]

    def at_y(place):
        return ((z * NY + place) * 2 + core, plane)

    def at_z(place):
        return ((place * NY + y) * 2 + core, plane)

    def across(step):
        return (seq, lax.rem(plane + step, NX))

    loads = [
        pltpu.make_async_copy(src, dst, in_sem.at[i])
        for i, (src, dst) in enumerate(
            ((k_hbm, k), (v_hbm, v), (q_hbm, q), (g_hbm, g), (gain_hbm, gain))
        )
    ]
    for load in loads:
        load.start()

    barrier = pltpu.get_barrier_semaphore()
    for place in z_peers:
        pl.semaphore_signal(barrier, inc=1, device_id=at_z(place), device_id_type=MESH)
    for place in y_peers:
        pl.semaphore_signal(barrier, inc=1, device_id=at_y(place), device_id_type=MESH)
    for step in range(1, NX):
        pl.semaphore_signal(barrier, inc=1, device_id=across(step), device_id_type=MESH)
    pl.semaphore_signal(barrier, inc=1, device_id=other, device_id_type=MESH)

    mine = core * HALF
    theirs = HALF - mine

    def cols(head):
        return pl.ds(pl.multiple_of(head * DH, DH), DH)

    def send(src, dst, sem, device):
        pltpu.make_async_remote_copy(
            src_ref=src,
            dst_ref=dst,
            send_sem=sem.at[0],
            recv_sem=sem.at[1],
            device_id=device,
            device_id_type=MESH,
        ).start()

    def swap_out(s, c, term):
        for j in range(PER):
            own[s, 1 - core, c, pl.ds(j * DH, DH)] = term(theirs + c * PER + j)
        send(own.at[s, 1 - core, c], swap.at[s, c], swap_sem.at[s, c], other)

    def y_out(s, c, term):
        for j in range(PER):
            own[s, core, c, pl.ds(j * DH, DH)] = term(mine + c * PER + j)
        wait_for(swap.at[s, c], swap_sem.at[s, c, 1])
        chip[s, c] = (own[s, core, c] + swap[s, c]).reshape(NY, YROWS, DH)
        for place in y_peers:
            send(chip.at[s, c, place], y_got.at[s, c, y], y_sem.at[s, c], at_y(place))
        y_got[s, c, y] = chip[s, c, y]

    def z_out(s, c):
        wait_for(y_got.at[s, c, pl.ds(0, NY - 1)], y_sem.at[s, c, 1])
        total = (y_got[s, c, 0] + y_got[s, c, 1]) + (y_got[s, c, 2] + y_got[s, c, 3])
        y_sum[s, c] = total.reshape(NZ, ZROWS, DH)
        for place in z_peers:
            send(y_sum.at[s, c, place], z_got.at[s, c, z], z_sem.at[s, c], at_z(place))
        z_got[s, c, z] = y_sum[s, c, z]

    def z_return(s, c, reverse):
        wait_for(z_got.at[s, c, pl.ds(0, NZ - 1)], z_sem.at[s, c, 1])
        total = jnp.zeros((ZROWS, DH), f32)
        for place in range(NZ - 1, -1, -1) if reverse else range(NZ):
            z_part[s, c, place] = total
            total = total + z_got[s, c, place]
        for place in z_peers:
            send(z_part.at[s, c, place], z_back.at[s, c, z], zb_sem.at[s, c], at_z(place))
        z_back[s, c, z] = z_part[s, c, z]

    def y_return(s, c, reverse):
        wait_for(z_back.at[s, c, pl.ds(0, NZ - 1)], zb_sem.at[s, c, 1])
        total = z_back[s, c].reshape(YROWS, DH)
        for place in range(NY - 1, -1, -1) if reverse else range(NY):
            y_part[s, c, place] = total
            total = total + y_got[s, c, place]
        for place in y_peers:
            send(y_part.at[s, c, place], y_back.at[s, c, y], yb_sem.at[s, c], at_y(place))
        y_back[s, c, y] = y_part[s, c, y]

    def collect(s, c, inner, use):
        wait_for(y_back.at[s, c, pl.ds(0, NY - 1)], yb_sem.at[s, c, 1])
        chip_part = y_back[s, c].reshape(PER * DH, DH)
        is_inner = core == inner
        both = chip_part + jnp.where(is_inner, own[s, core, c], swap[s, c])
        ahead[s, c] = jnp.where(is_inner, both, chip_part)
        send(ahead.at[s, c], arrived.at[s, c], ahead_sem.at[s, c], other)
        result = jnp.where(is_inner, chip_part, both).astype(bf16)
        for j in range(PER):
            use(mine + c * PER + j, result[j * DH:(j + 1) * DH])

    def collect_theirs(s, c, use):
        wait_for(arrived.at[s, c], ahead_sem.at[s, c, 1])
        result = arrived[s, c].astype(bf16)
        for j in range(PER):
            use(theirs + c * PER + j, result[j * DH:(j + 1) * DH])

    def finish_sends(s):
        for c in range(CHUNKS):
            wait_for(swap.at[s, c], swap_sem.at[s, c, 0])
            wait_for(y_got.at[s, c, pl.ds(0, NY - 1)], y_sem.at[s, c, 0])
            wait_for(z_got.at[s, c, pl.ds(0, NZ - 1)], z_sem.at[s, c, 0])
            wait_for(z_back.at[s, c, pl.ds(0, NZ - 1)], zb_sem.at[s, c, 0])
            wait_for(y_back.at[s, c, pl.ds(0, NY - 1)], yb_sem.at[s, c, 0])
            wait_for(arrived.at[s, c], ahead_sem.at[s, c, 0])

    def heads(first, count, body):
        def pair(i, carry):
            body(first + 2 * i)
            body(first + 2 * i + 1)
            return carry

        lax.fori_loop(0, count // 2, pair, 0)

    chunks = range(CHUNKS)
    rows = lax.broadcasted_iota(jnp.int32, (GROUP, GROUP), 0)
    columns = lax.broadcasted_iota(jnp.int32, (GROUP, GROUP), 1)
    causal = rows >= columns

    def key_value(head):
        return dot(k[:, cols(head)], v[:, cols(head)], 0, 0)

    loads[0].wait()
    loads[1].wait()
    pl.semaphore_wait(barrier, PEERS)
    for c in chunks:
        swap_out(0, c, key_value)
    for c in chunks:
        y_out(0, c, key_value)
    for load in loads[2:]:
        load.wait()

    def within(head):
        at = cols(head)
        part = dot(q[:, at], k[:, at], 1, 1)
        masked = jnp.where(causal, part, 0.0).astype(bf16)
        scores[head] = masked
        attn[:, at] = dot(masked, v[:, at], 1, 0)

    def prepare(i, carry):
        for head in (2 * i, 2 * i + 1):
            q_t[head] = q[:, cols(head)].T
        at = pl.ds(pl.multiple_of(i * 2 * DH, 2 * DH), 2 * DH)
        scaled[:, at] = gain[at].astype(f32).reshape(1, 2 * DH) * g[:, at].astype(f32)
        return carry

    heads(0, HALF, within)
    for c in chunks:
        z_out(0, c)
    heads(HALF, HALF, within)
    for c in chunks:
        z_return(0, c, False)
    lax.fori_loop(0, HEADS // 2, prepare, 0)
    for c in chunks:
        y_return(0, c, False)
    norm_acc[...] = jnp.zeros_like(norm_acc)

    def finish_attn(head, state_b):
        at = cols(head)
        state[head] = state_b
        value = attn[:, at] + dot(q[:, at], state_b, 1, 0)
        attn[:, at] = value
        norm_acc[0] += value * value
        norm_acc[1] += scaled[:, at] * value

    for c in chunks:
        collect(0, c, 0, finish_attn)
    for c in chunks:
        collect_theirs(0, c, finish_attn)

    norm_got[plane, 0:1] = jnp.sum(norm_acc[0].T, axis=0, keepdims=True)
    norm_got[plane, 1:2] = jnp.sum(norm_acc[1].T, axis=0, keepdims=True)
    for step in (2, 1, 3):
        send(norm_got.at[plane], norm_got.at[plane], norm_sem, across(step))
    wait_for(norm_got.at[pl.ds(0, NX - 1)], norm_sem.at[1])
    sums = (norm_got[0] + norm_got[1]) + (norm_got[2] + norm_got[3])
    features = float(NX * HEADS * DH)
    inverse = lax.rsqrt(sums[0:1] / features + 1e-05)
    weight = inverse * inverse * inverse * (sums[1:2] / features)
    wait_for(norm_got.at[pl.ds(0, NX - 1)], norm_sem.at[0])
    norm_acc[0] = jnp.broadcast_to(inverse, (DH, GROUP)).T
    norm_acc[1] = jnp.broadcast_to(weight, (DH, GROUP)).T

    def query_delta(head):
        at = cols(head)
        value = (norm_acc[0] * scaled[:, at] - attn[:, at] * norm_acc[1]).astype(bf16)
        delta[:, at] = value
        return dot(q_t[head], value, 1, 0)

    for c in chunks:
        swap_out(1, c, query_delta)
    for c in chunks:
        y_out(1, c, query_delta)

    def query_side(head):
        at = cols(head)
        part = dot(delta[:, at], v[:, at], 1, 1)
        masked = jnp.where(causal, part, 0.0).astype(bf16)
        dscore[head] = masked
        grad = dot(masked, k[:, at], 1, 0) + dot(delta[:, at], state[head], 1, 1)
        qg[:, at] = grad.astype(bf16)

    def key_side(head):
        at = cols(head)
        kg_part[:, at] = dot(dscore[head], q[:, at], 0, 0)
        vg_part[:, at] = dot(scores[head], delta[:, at], 0, 0)

    heads(0, HALF, query_side)
    for c in chunks:
        z_out(1, c)
    heads(HALF, HALF, query_side)
    for c in chunks:
        z_return(1, c, True)
    heads(0, HALF, key_side)
    for c in chunks:
        y_return(1, c, True)
    heads(HALF, HALF, key_side)

    def finish_keys(head, later_b):
        at = cols(head)
        kg[:, at] = (kg_part[:, at] + dot(v[:, at], later_b, 1, 1)).astype(bf16)
        vg[:, at] = (vg_part[:, at] + dot(k[:, at], later_b, 1, 0)).astype(bf16)

    for c in chunks:
        collect(1, c, 1, finish_keys)
    for c in chunks:
        collect_theirs(1, c, finish_keys)
    finish_sends(0)
    finish_sends(1)


def shards(queries, keys, values, out_grad, norm_gain):
    tokens, width = queries.shape
    vmem = pltpu.VMEM
    grad = jax.ShapeDtypeStruct((tokens, width), bf16)
    hbm = pl.BlockSpec(memory_space=pltpu.HBM)
    on_chip = pl.BlockSpec(memory_space=pltpu.VMEM)
    dma = pltpu.SemaphoreType.DMA
    flat = (2, CHUNKS, PER * DH, DH)
    by_y = (2, CHUNKS, NY, YROWS, DH)
    by_z = (2, CHUNKS, NZ, ZROWS, DH)
    pairs = (2, CHUNKS, 2)
    return pl.pallas_call(
        kernel,
        out_shape=(grad, grad, grad),
        in_specs=[hbm, hbm, hbm, hbm, hbm],
        out_specs=(on_chip, on_chip, on_chip),
        scratch_shapes=[
            vmem((tokens, width), bf16),
            vmem((tokens, width), bf16),
            vmem((tokens, width), bf16),
            vmem((tokens, width), bf16),
            vmem((width,), bf16),
            vmem((HEADS, DH, GROUP), bf16),
            vmem((tokens, width), f32),
            vmem((tokens, width), f32),
            vmem((tokens, width), bf16),
            vmem((HEADS, GROUP, GROUP), bf16),
            vmem((HEADS, GROUP, GROUP), bf16),
            vmem((tokens, width), f32),
            vmem((tokens, width), f32),
            vmem((HEADS, DH, DH), bf16),
            vmem((2, 2, CHUNKS, PER * DH, DH), f32),
            vmem(flat, f32),
            vmem(by_y, f32),
            vmem(by_y, f32),
            vmem(by_z, f32),
            vmem(by_z, f32),
            vmem(by_z, f32),
            vmem(by_z, f32),
            vmem(by_y, f32),
            vmem(by_y, f32),
            vmem(flat, f32),
            vmem(flat, f32),
            vmem((2, GROUP, DH), f32),
            vmem((NX, 8, GROUP), f32),
            dma((5,)),
            dma(pairs),
            dma(pairs),
            dma(pairs),
            dma(pairs),
            dma(pairs),
            dma(pairs),
            dma((2,)),
        ],
        compiler_params=pltpu.CompilerParams(
            collective_id=0, has_side_effects=True, vmem_limit_bytes=46 * 2**20
        ),
        name="block_backward",
    )(
        *(
            pltpu.with_memory_space_constraint(arg, pltpu.HBM)
            for arg in (queries, keys, values, out_grad, norm_gain)
        )
    )


def solution(mesh):
    return jax.shard_map(
        shards,
        mesh=mesh,
        in_specs=(
            P("seq", "head"),
            P("seq", "head"),
            P("seq", "head"),
            P("seq", "head"),
            P("head"),
        ),
        out_specs=(P("seq", "head"), P("seq", "head"), P("seq", "head")),
        check_vma=False,
    )
```

```python
import functools

import jax
import jax.numpy as jnp
from jax import lax
from jax.experimental import pallas as pl
from jax.experimental.pallas import tpu as pltpu
from jax.sharding import PartitionSpec as P

DH = 128
GROUP = 256
HEADS = 16
HALF = 8
NZ = 8
NY = 4
NX = 4
CHUNKS = 4
PER = HALF // CHUNKS
YROWS = PER * DH // NY
ZROWS = YROWS // NZ
MESH = pl.DeviceIdType.MESH
FAR_Z = (4, 3, 5, 2, 6, 1, 7)
FAR_Y = (2, 1, 3)
FIRST = (
    "y0", "y1", "y2", "y3", "w", "w", "w", "z0", "z1", "z2", "z3", "w", "w", "r0", "r1", "r2",
    "r3", "w", "b0", "b1", "b2", "b3", "c0", "c1", "t0", "c2", "t1", "c3", "t2", "t3",
)
SECOND = (
    "s0", "s1", "y0", "s2", "y1", "s3", "y2", "y3", "w", "w", "z0", "z1", "z2", "z3", "w", "w",
    "r0", "r1", "r2", "r3", "w", "w", "b0", "b1", "b2", "b3", "w", "w", "c0", "c1", "t0", "c2",
    "t1", "c3", "t2", "t3",
)
PEERS = 1 + len(FAR_Z) + len(FAR_Y) + NX - 1

f32 = jnp.float32
bf16 = jnp.bfloat16


def dot(a, b, dim_a, dim_b):
    return lax.dot_general(
        a, b, (((dim_a,), (dim_b,)), ((), ())), preferred_element_type=f32
    )


def wait_for(ref, sem):
    pltpu.make_async_copy(ref, ref, sem).wait()


def kernel(
    q_hbm, k_hbm, v_hbm, g_hbm, gain_hbm,
    qg, kg, vg,
    q, k, v, g, gain, q_t, attn, scaled, delta, scores, dscore, kg_part, vg_part, state,
    own, swap, chip, y_got, y_sum, z_got, z_part, z_back, y_part, y_back, ahead, arrived,
    norm_acc, norm_got,
    in_sem, swap_sem, y_sem, z_sem, zb_sem, yb_sem, ahead_sem, norm_sem,
):
    seq = lax.axis_index("seq")
    plane = lax.axis_index("head")
    core = lax.rem(seq, 2)
    z, y = seq // (2 * NY), lax.rem(seq // 2, NY)
    other = (seq + 1 - 2 * core, plane)
    y_peers = [lax.rem(y + step, NY) for step in FAR_Y]
    z_peers = [lax.rem(z + step, NZ) for step in FAR_Z]

    def at_y(place):
        return ((z * NY + place) * 2 + core, plane)

    def at_z(place):
        return ((place * NY + y) * 2 + core, plane)

    def across(step):
        return (seq, lax.rem(plane + step, NX))

    loads = [
        pltpu.make_async_copy(src, dst, in_sem.at[i])
        for i, (src, dst) in enumerate(
            ((k_hbm, k), (v_hbm, v), (q_hbm, q), (g_hbm, g), (gain_hbm, gain))
        )
    ]
    for load in loads[:2]:
        load.start()

    barrier = pltpu.get_barrier_semaphore()
    for place in z_peers:
        pl.semaphore_signal(barrier, inc=1, device_id=at_z(place), device_id_type=MESH)
    for place in y_peers:
        pl.semaphore_signal(barrier, inc=1, device_id=at_y(place), device_id_type=MESH)
    for step in range(1, NX):
        pl.semaphore_signal(barrier, inc=1, device_id=across(step), device_id_type=MESH)
    pl.semaphore_signal(barrier, inc=1, device_id=other, device_id_type=MESH)

    mine = core * HALF
    theirs = HALF - mine

    def cols(head):
        return pl.ds(pl.multiple_of(head * DH, DH), DH)

    def send(src, dst, sem, device):
        pltpu.make_async_remote_copy(
            src_ref=src,
            dst_ref=dst,
            send_sem=sem.at[0],
            recv_sem=sem.at[1],
            device_id=device,
            device_id_type=MESH,
        ).start()

    def fill(s, c, term):
        for j in range(PER):
            own[s, 1 - core, c, pl.ds(j * DH, DH)] = term(theirs + c * PER + j)

    def swap_out(s, c):
        send(own.at[s, 1 - core, c], swap.at[s, c], swap_sem.at[s, c], other)

    def y_out(s, c, term):
        for j in range(PER):
            own[s, core, c, pl.ds(j * DH, DH)] = term(mine + c * PER + j)
        wait_for(swap.at[s, c], swap_sem.at[s, c, 1])
        chip[s, c] = (own[s, core, c] + swap[s, c]).reshape(NY, YROWS, DH)
        for place in y_peers:
            send(chip.at[s, c, place], y_got.at[s, c, y], y_sem.at[s, c], at_y(place))
        y_got[s, c, y] = chip[s, c, y]

    def z_out(s, c):
        wait_for(y_got.at[s, c, pl.ds(0, NY - 1)], y_sem.at[s, c, 1])
        total = (y_got[s, c, 0] + y_got[s, c, 1]) + (y_got[s, c, 2] + y_got[s, c, 3])
        y_sum[s, c] = total.reshape(NZ, ZROWS, DH)
        for place in z_peers:
            send(y_sum.at[s, c, place], z_got.at[s, c, z], z_sem.at[s, c], at_z(place))
        z_got[s, c, z] = y_sum[s, c, z]

    def z_return(s, c, reverse):
        wait_for(z_got.at[s, c, pl.ds(0, NZ - 1)], z_sem.at[s, c, 1])
        total = jnp.zeros((ZROWS, DH), f32)
        for place in range(NZ - 1, -1, -1) if reverse else range(NZ):
            z_part[s, c, place] = total
            total = total + z_got[s, c, place]
        for place in z_peers:
            send(z_part.at[s, c, place], z_back.at[s, c, z], zb_sem.at[s, c], at_z(place))
        z_back[s, c, z] = z_part[s, c, z]

    def y_return(s, c, reverse):
        wait_for(z_back.at[s, c, pl.ds(0, NZ - 1)], zb_sem.at[s, c, 1])
        total = z_back[s, c].reshape(YROWS, DH)
        for place in range(NY - 1, -1, -1) if reverse else range(NY):
            y_part[s, c, place] = total
            total = total + y_got[s, c, place]
        for place in y_peers:
            send(y_part.at[s, c, place], y_back.at[s, c, y], yb_sem.at[s, c], at_y(place))
        y_back[s, c, y] = y_part[s, c, y]

    def collect(s, c, inner, use):
        wait_for(y_back.at[s, c, pl.ds(0, NY - 1)], yb_sem.at[s, c, 1])
        chip_part = y_back[s, c].reshape(PER * DH, DH)
        is_inner = core == inner
        both = chip_part + jnp.where(is_inner, own[s, core, c], swap[s, c])
        ahead[s, c] = jnp.where(is_inner, both, chip_part)
        send(ahead.at[s, c], arrived.at[s, c], ahead_sem.at[s, c], other)
        result = jnp.where(is_inner, chip_part, both).astype(bf16)
        for j in range(PER):
            use(mine + c * PER + j, result[j * DH:(j + 1) * DH])

    def collect_theirs(s, c, use):
        wait_for(arrived.at[s, c], ahead_sem.at[s, c, 1])
        result = arrived[s, c].astype(bf16)
        for j in range(PER):
            use(theirs + c * PER + j, result[j * DH:(j + 1) * DH])

    def finish_sends(s):
        for c in range(CHUNKS):
            wait_for(swap.at[s, c], swap_sem.at[s, c, 0])
            wait_for(y_got.at[s, c, pl.ds(0, NY - 1)], y_sem.at[s, c, 0])
            wait_for(z_got.at[s, c, pl.ds(0, NZ - 1)], z_sem.at[s, c, 0])
            wait_for(z_back.at[s, c, pl.ds(0, NZ - 1)], zb_sem.at[s, c, 0])
            wait_for(y_back.at[s, c, pl.ds(0, NY - 1)], yb_sem.at[s, c, 0])
            wait_for(arrived.at[s, c], ahead_sem.at[s, c, 0])

    def run(order, s, reverse, term, inner, use, local):
        local = list(local)
        for step in order:
            name, c = step[0], int(step[1:] or 0)
            if name == "s":
                fill(s, c, term)
                swap_out(s, c)
            elif name == "y":
                y_out(s, c, term)
            elif name == "z":
                z_out(s, c)
            elif name == "r":
                z_return(s, c, reverse)
            elif name == "b":
                y_return(s, c, reverse)
            elif name == "c":
                collect(s, c, inner, use)
            elif name == "t":
                collect_theirs(s, c, use)
            else:
                local.pop(0)()
        assert not local

    def heads(first, count, body):
        def pair(i, carry):
            body(first + 2 * i)
            body(first + 2 * i + 1)
            return carry

        lax.fori_loop(0, count // 2, pair, 0)

    chunks = range(CHUNKS)
    rows = lax.broadcasted_iota(jnp.int32, (GROUP, GROUP), 0)
    columns = lax.broadcasted_iota(jnp.int32, (GROUP, GROUP), 1)
    causal = rows >= columns

    def key_value(head):
        return dot(k[:, cols(head)], v[:, cols(head)], 0, 0)

    loads[0].wait()
    loads[1].wait()
    for c in chunks:
        fill(0, c, key_value)
    for load in loads[2:]:
        load.start()
    pl.semaphore_wait(barrier, PEERS)
    for c in chunks:
        swap_out(0, c)

    def within(head):
        at = cols(head)
        part = dot(q[:, at], k[:, at], 1, 1)
        masked = jnp.where(causal, part, 0.0).astype(bf16)
        scores[head] = masked
        attn[:, at] = dot(masked, v[:, at], 1, 0)

    def prepare(i, carry):
        for head in (2 * i, 2 * i + 1):
            q_t[head] = q[:, cols(head)].T
        at = pl.ds(pl.multiple_of(i * 2 * DH, 2 * DH), 2 * DH)
        scaled[:, at] = gain[at].astype(f32).reshape(1, 2 * DH) * g[:, at].astype(f32)
        return carry

    norm_acc[...] = jnp.zeros_like(norm_acc)

    def finish_attn(head, state_b):
        at = cols(head)
        state[head] = state_b
        value = attn[:, at] + dot(q[:, at], state_b, 1, 0)
        attn[:, at] = value
        norm_acc[0] += value * value
        norm_acc[1] += scaled[:, at] * value

    def load_rest():
        for load in loads[2:]:
            load.wait()

    run(
        FIRST, 0, False, key_value, 0, finish_attn,
        [load_rest]
        + [functools.partial(heads, i, 4, within) for i in range(0, HEADS, 4)]
        + [lambda: lax.fori_loop(0, HEADS // 2, prepare, 0)],
    )

    norm_got[plane, 0:1] = jnp.sum(norm_acc[0].T, axis=0, keepdims=True)
    norm_got[plane, 1:2] = jnp.sum(norm_acc[1].T, axis=0, keepdims=True)
    for step in (2, 1, 3):
        send(norm_got.at[plane], norm_got.at[plane], norm_sem, across(step))
    wait_for(norm_got.at[pl.ds(0, NX - 1)], norm_sem.at[1])
    sums = (norm_got[0] + norm_got[1]) + (norm_got[2] + norm_got[3])
    features = float(NX * HEADS * DH)
    inverse = lax.rsqrt(sums[0:1] / features + 1e-05)
    weight = inverse * inverse * inverse * (sums[1:2] / features)
    norm_acc[0] = jnp.broadcast_to(inverse, (DH, GROUP)).T
    norm_acc[1] = jnp.broadcast_to(weight, (DH, GROUP)).T

    def query_delta(head):
        at = cols(head)
        value = (norm_acc[0] * scaled[:, at] - attn[:, at] * norm_acc[1]).astype(bf16)
        delta[:, at] = value
        return dot(q_t[head], value, 1, 0)

    def query_side(head):
        at = cols(head)
        part = dot(delta[:, at], v[:, at], 1, 1)
        masked = jnp.where(causal, part, 0.0).astype(bf16)
        dscore[head] = masked
        grad = dot(masked, k[:, at], 1, 0) + dot(delta[:, at], state[head], 1, 1)
        qg[:, at] = grad.astype(bf16)

    def key_side(head):
        at = cols(head)
        kg_part[:, at] = dot(dscore[head], q[:, at], 0, 0)
        vg_part[:, at] = dot(scores[head], delta[:, at], 0, 0)

    def finish_keys(head, later_b):
        at = cols(head)
        kg[:, at] = (kg_part[:, at] + dot(v[:, at], later_b, 1, 1)).astype(bf16)
        vg[:, at] = (vg_part[:, at] + dot(k[:, at], later_b, 1, 0)).astype(bf16)

    run(
        SECOND, 1, True, query_delta, 1, finish_keys,
        [functools.partial(heads, i, 4, query_side) for i in range(0, HEADS, 4)]
        + [functools.partial(heads, i, 4, key_side) for i in range(0, HEADS, 4)],
    )
    wait_for(norm_got.at[pl.ds(0, NX - 1)], norm_sem.at[0])
    finish_sends(0)
    finish_sends(1)


def write_out(a, b, c, a_out, b_out, c_out, sem):
    copies = [
        pltpu.make_async_copy(src, dst, sem.at[i])
        for i, (src, dst) in enumerate(((a, a_out), (b, b_out), (c, c_out)))
    ]
    for copy in copies:
        copy.start()
    for copy in copies:
        copy.wait()


def shards(queries, keys, values, out_grad, norm_gain):
    tokens, width = queries.shape
    vmem = pltpu.VMEM
    grad = jax.ShapeDtypeStruct((tokens, width), bf16)
    hbm = pl.BlockSpec(memory_space=pltpu.HBM)
    on_chip = pl.BlockSpec(memory_space=pltpu.VMEM)
    dma = pltpu.SemaphoreType.DMA
    flat = (2, CHUNKS, PER * DH, DH)
    by_y = (2, CHUNKS, NY, YROWS, DH)
    by_z = (2, CHUNKS, NZ, ZROWS, DH)
    pairs = (2, CHUNKS, 2)
    results = pl.pallas_call(
        kernel,
        out_shape=(grad, grad, grad),
        in_specs=[hbm, hbm, hbm, hbm, hbm],
        out_specs=(on_chip, on_chip, on_chip),
        scratch_shapes=[
            vmem((tokens, width), bf16),
            vmem((tokens, width), bf16),
            vmem((tokens, width), bf16),
            vmem((tokens, width), bf16),
            vmem((width,), bf16),
            vmem((HEADS, DH, GROUP), bf16),
            vmem((tokens, width), f32),
            vmem((tokens, width), f32),
            vmem((tokens, width), bf16),
            vmem((HEADS, GROUP, GROUP), bf16),
            vmem((HEADS, GROUP, GROUP), bf16),
            vmem((tokens, width), f32),
            vmem((tokens, width), f32),
            vmem((HEADS, DH, DH), bf16),
            vmem((2, 2, CHUNKS, PER * DH, DH), f32),
            vmem(flat, f32),
            vmem(by_y, f32),
            vmem(by_y, f32),
            vmem(by_z, f32),
            vmem(by_z, f32),
            vmem(by_z, f32),
            vmem(by_z, f32),
            vmem(by_y, f32),
            vmem(by_y, f32),
            vmem(flat, f32),
            vmem(flat, f32),
            vmem((2, GROUP, DH), f32),
            vmem((NX, 8, GROUP), f32),
            dma((5,)),
            dma(pairs),
            dma(pairs),
            dma(pairs),
            dma(pairs),
            dma(pairs),
            dma(pairs),
            dma((2,)),
        ],
        compiler_params=pltpu.CompilerParams(
            collective_id=0, has_side_effects=True, vmem_limit_bytes=46 * 2**20
        ),
        name="block_backward",
    )(
        *(
            pltpu.with_memory_space_constraint(arg, pltpu.HBM)
            for arg in (queries, keys, values, out_grad, norm_gain)
        )
    )
    return pl.pallas_call(
        write_out,
        out_shape=(grad, grad, grad),
        in_specs=[on_chip, on_chip, on_chip],
        out_specs=(hbm, hbm, hbm),
        scratch_shapes=[dma((3,))],
        compiler_params=pltpu.CompilerParams(vmem_limit_bytes=4 * 2**20),
        name="stage_out",
    )(*results)


def solution(mesh):
    return jax.shard_map(
        shards,
        mesh=mesh,
        in_specs=(
            P("seq", "head"),
            P("seq", "head"),
            P("seq", "head"),
            P("seq", "head"),
            P("head"),
        ),
        out_specs=(P("seq", "head"), P("seq", "head"), P("seq", "head")),
        check_vma=False,
    )
```

```python
import functools

import jax
import jax.numpy as jnp
from jax import lax
from jax.experimental import pallas as pl
from jax.experimental.pallas import tpu as pltpu
from jax.sharding import PartitionSpec as P

DH = 128
GROUP = 256
HEADS = 16
HALF = 8
NZ = 8
NY = 4
NX = 4
CHUNKS = 4
PER = HALF // CHUNKS
YROWS = PER * DH // NY
ZROWS = YROWS // NZ
MESH = pl.DeviceIdType.MESH
FAR_Z = (4, 3, 5, 2, 6, 1, 7)
FAR_Y = (2, 1, 3)
FIRST = (
    "y0", "y1", "y2", "y3", "w", "w", "w", "z0", "z1", "z2", "r0", "z3", "w", "w", "r1", "r2", "b0",
    "r3", "w", "b1", "b2", "b3", "c0", "c1", "t0", "c2", "t1", "c3", "t2", "t3",
)
SECOND = (
    "s0", "s1", "y0", "s2", "y1", "s3", "y2", "y3", "w", "w", "z0", "z1", "z2", "r0", "z3", "w", "w",
    "r1", "r2", "b0", "r3", "w", "w", "b1", "b2", "b3", "w", "w", "c0", "c1", "t0", "c2",
    "t1", "c3", "t2", "t3",
)
PEERS = 1 + len(FAR_Z) + len(FAR_Y) + NX - 1

f32 = jnp.float32
bf16 = jnp.bfloat16


def dot(a, b, dim_a, dim_b):
    return lax.dot_general(
        a, b, (((dim_a,), (dim_b,)), ((), ())), preferred_element_type=f32
    )


def wait_for(ref, sem):
    pltpu.make_async_copy(ref, ref, sem).wait()


def kernel(
    q_hbm, k_hbm, v_hbm, g_hbm, gain_hbm,
    qg, kg, vg,
    q, k, v, g, gain, q_t, attn, scaled, delta, scores, dscore, kg_part, vg_part, state,
    own, swap, chip, y_got, y_sum, z_got, z_part, z_back, y_part, y_back, ahead, arrived,
    norm_acc, norm_got,
    in_sem, swap_sem, y_sem, z_sem, zb_sem, yb_sem, ahead_sem, norm_sem,
):
    seq = lax.axis_index("seq")
    plane = lax.axis_index("head")
    core = lax.rem(seq, 2)
    z, y = seq // (2 * NY), lax.rem(seq // 2, NY)
    other = (seq + 1 - 2 * core, plane)
    y_peers = [lax.rem(y + step, NY) for step in FAR_Y]
    z_peers = [lax.rem(z + step, NZ) for step in FAR_Z]

    def at_y(place):
        return ((z * NY + place) * 2 + core, plane)

    def at_z(place):
        return ((place * NY + y) * 2 + core, plane)

    def across(step):
        return (seq, lax.rem(plane + step, NX))

    loads = [
        pltpu.make_async_copy(src, dst, in_sem.at[i])
        for i, (src, dst) in enumerate(
            ((k_hbm, k), (v_hbm, v), (q_hbm, q), (g_hbm, g), (gain_hbm, gain))
        )
    ]
    for load in loads[:2]:
        load.start()

    barrier = pltpu.get_barrier_semaphore()
    for place in z_peers:
        pl.semaphore_signal(barrier, inc=1, device_id=at_z(place), device_id_type=MESH)
    for place in y_peers:
        pl.semaphore_signal(barrier, inc=1, device_id=at_y(place), device_id_type=MESH)
    for step in range(1, NX):
        pl.semaphore_signal(barrier, inc=1, device_id=across(step), device_id_type=MESH)
    pl.semaphore_signal(barrier, inc=1, device_id=other, device_id_type=MESH)

    mine = core * HALF
    theirs = HALF - mine

    def cols(head):
        return pl.ds(pl.multiple_of(head * DH, DH), DH)

    def send(src, dst, sem, device):
        pltpu.make_async_remote_copy(
            src_ref=src,
            dst_ref=dst,
            send_sem=sem.at[0],
            recv_sem=sem.at[1],
            device_id=device,
            device_id_type=MESH,
        ).start()

    def fill(s, c, term):
        for j in range(PER):
            own[s, 1 - core, c, pl.ds(j * DH, DH)] = term(theirs + c * PER + j)

    def swap_out(s, c):
        send(own.at[s, 1 - core, c], swap.at[s, c], swap_sem.at[s, c], other)

    def y_out(s, c, term):
        for j in range(PER):
            own[s, core, c, pl.ds(j * DH, DH)] = term(mine + c * PER + j)
        wait_for(swap.at[s, c], swap_sem.at[s, c, 1])
        chip[s, c] = (own[s, core, c] + swap[s, c]).reshape(NY, YROWS, DH)
        for place in y_peers:
            send(chip.at[s, c, place], y_got.at[s, c, y], y_sem.at[s, c], at_y(place))
        y_got[s, c, y] = chip[s, c, y]

    def z_out(s, c):
        wait_for(y_got.at[s, c, pl.ds(0, NY - 1)], y_sem.at[s, c, 1])
        total = (y_got[s, c, 0] + y_got[s, c, 1]) + (y_got[s, c, 2] + y_got[s, c, 3])
        y_sum[s, c] = total.reshape(NZ, ZROWS, DH)
        for place in z_peers:
            send(y_sum.at[s, c, place], z_got.at[s, c, z], z_sem.at[s, c], at_z(place))
        z_got[s, c, z] = y_sum[s, c, z]

    def z_return(s, c, reverse):
        wait_for(z_got.at[s, c, pl.ds(0, NZ - 1)], z_sem.at[s, c, 1])
        total = jnp.zeros((ZROWS, DH), f32)
        for place in range(NZ - 1, -1, -1) if reverse else range(NZ):
            z_part[s, c, place] = total
            total = total + z_got[s, c, place]
        for place in z_peers:
            send(z_part.at[s, c, place], z_back.at[s, c, z], zb_sem.at[s, c], at_z(place))
        z_back[s, c, z] = z_part[s, c, z]

    def y_return(s, c, reverse):
        wait_for(z_back.at[s, c, pl.ds(0, NZ - 1)], zb_sem.at[s, c, 1])
        total = z_back[s, c].reshape(YROWS, DH)
        for place in range(NY - 1, -1, -1) if reverse else range(NY):
            y_part[s, c, place] = total
            total = total + y_got[s, c, place]
        for place in y_peers:
            send(y_part.at[s, c, place], y_back.at[s, c, y], yb_sem.at[s, c], at_y(place))
        y_back[s, c, y] = y_part[s, c, y]

    def collect(s, c, inner, use):
        wait_for(y_back.at[s, c, pl.ds(0, NY - 1)], yb_sem.at[s, c, 1])
        chip_part = y_back[s, c].reshape(PER * DH, DH)
        is_inner = core == inner
        both = chip_part + jnp.where(is_inner, own[s, core, c], swap[s, c])
        ahead[s, c] = jnp.where(is_inner, both, chip_part)
        send(ahead.at[s, c], arrived.at[s, c], ahead_sem.at[s, c], other)
        result = jnp.where(is_inner, chip_part, both).astype(bf16)
        for j in range(PER):
            use(mine + c * PER + j, result[j * DH:(j + 1) * DH])

    def collect_theirs(s, c, use):
        wait_for(arrived.at[s, c], ahead_sem.at[s, c, 1])
        result = arrived[s, c].astype(bf16)
        for j in range(PER):
            use(theirs + c * PER + j, result[j * DH:(j + 1) * DH])

    def finish_sends(s):
        for c in range(CHUNKS):
            wait_for(swap.at[s, c], swap_sem.at[s, c, 0])
            wait_for(y_got.at[s, c, pl.ds(0, NY - 1)], y_sem.at[s, c, 0])
            wait_for(z_got.at[s, c, pl.ds(0, NZ - 1)], z_sem.at[s, c, 0])
            wait_for(z_back.at[s, c, pl.ds(0, NZ - 1)], zb_sem.at[s, c, 0])
            wait_for(y_back.at[s, c, pl.ds(0, NY - 1)], yb_sem.at[s, c, 0])
            wait_for(arrived.at[s, c], ahead_sem.at[s, c, 0])

    def run(order, s, reverse, term, inner, use, local):
        local = list(local)
        for step in order:
            name, c = step[0], int(step[1:] or 0)
            if name == "s":
                fill(s, c, term)
                swap_out(s, c)
            elif name == "y":
                y_out(s, c, term)
            elif name == "z":
                z_out(s, c)
            elif name == "r":
                z_return(s, c, reverse)
            elif name == "b":
                y_return(s, c, reverse)
            elif name == "c":
                collect(s, c, inner, use)
            elif name == "t":
                collect_theirs(s, c, use)
            else:
                local.pop(0)()
        assert not local

    def heads(first, count, body):
        def pair(i, carry):
            body(first + 2 * i)
            body(first + 2 * i + 1)
            return carry

        lax.fori_loop(0, count // 2, pair, 0)

    chunks = range(CHUNKS)
    rows = lax.broadcasted_iota(jnp.int32, (GROUP, GROUP), 0)
    columns = lax.broadcasted_iota(jnp.int32, (GROUP, GROUP), 1)
    causal = rows >= columns

    def key_value(head):
        return dot(k[:, cols(head)], v[:, cols(head)], 0, 0)

    loads[0].wait()
    loads[1].wait()
    for c in chunks:
        fill(0, c, key_value)
    for load in loads[2:]:
        load.start()
    pl.semaphore_wait(barrier, PEERS)
    for c in chunks:
        swap_out(0, c)

    def within(head):
        at = cols(head)
        part = dot(q[:, at], k[:, at], 1, 1)
        masked = jnp.where(causal, part, 0.0).astype(bf16)
        scores[head] = masked
        attn[:, at] = dot(masked, v[:, at], 1, 0)

    def prepare(i, carry):
        for head in (2 * i, 2 * i + 1):
            q_t[head] = q[:, cols(head)].T
        at = pl.ds(pl.multiple_of(i * 2 * DH, 2 * DH), 2 * DH)
        scaled[:, at] = gain[at].astype(f32).reshape(1, 2 * DH) * g[:, at].astype(f32)
        return carry

    norm_acc[...] = jnp.zeros_like(norm_acc)

    def finish_attn(head, state_b):
        at = cols(head)
        state[head] = state_b
        value = attn[:, at] + dot(q[:, at], state_b, 1, 0)
        attn[:, at] = value
        norm_acc[0] += value * value
        norm_acc[1] += scaled[:, at] * value

    def load_rest():
        for load in loads[2:]:
            load.wait()

    run(
        FIRST, 0, False, key_value, 0, finish_attn,
        [load_rest]
        + [functools.partial(heads, i, 4, within) for i in range(0, HEADS, 4)]
        + [lambda: lax.fori_loop(0, HEADS // 2, prepare, 0)],
    )

    norm_got[plane, 0:1] = jnp.sum(norm_acc[0].T, axis=0, keepdims=True)
    norm_got[plane, 1:2] = jnp.sum(norm_acc[1].T, axis=0, keepdims=True)
    for step in (2, 1, 3):
        send(norm_got.at[plane], norm_got.at[plane], norm_sem, across(step))
    wait_for(norm_got.at[pl.ds(0, NX - 1)], norm_sem.at[1])
    sums = (norm_got[0] + norm_got[1]) + (norm_got[2] + norm_got[3])
    features = float(NX * HEADS * DH)
    inverse = lax.rsqrt(sums[0:1] / features + 1e-05)
    weight = inverse * inverse * inverse * (sums[1:2] / features)
    norm_acc[0] = jnp.broadcast_to(inverse, (DH, GROUP)).T
    norm_acc[1] = jnp.broadcast_to(weight, (DH, GROUP)).T

    def query_delta(head):
        at = cols(head)
        value = (norm_acc[0] * scaled[:, at] - attn[:, at] * norm_acc[1]).astype(bf16)
        delta[:, at] = value
        return dot(q_t[head], value, 1, 0)

    def query_side(head):
        at = cols(head)
        part = dot(delta[:, at], v[:, at], 1, 1)
        masked = jnp.where(causal, part, 0.0).astype(bf16)
        dscore[head] = masked
        grad = dot(masked, k[:, at], 1, 0) + dot(delta[:, at], state[head], 1, 1)
        qg[:, at] = grad.astype(bf16)

    def key_side(head):
        at = cols(head)
        kg_part[:, at] = dot(dscore[head], q[:, at], 0, 0)
        vg_part[:, at] = dot(scores[head], delta[:, at], 0, 0)

    def finish_keys(head, later_b):
        at = cols(head)
        kg[:, at] = (kg_part[:, at] + dot(v[:, at], later_b, 1, 1)).astype(bf16)
        vg[:, at] = (vg_part[:, at] + dot(k[:, at], later_b, 1, 0)).astype(bf16)

    run(
        SECOND, 1, True, query_delta, 1, finish_keys,
        [functools.partial(heads, i, 4, query_side) for i in range(0, HEADS, 4)]
        + [functools.partial(heads, i, 4, key_side) for i in range(0, HEADS, 4)],
    )
    wait_for(norm_got.at[pl.ds(0, NX - 1)], norm_sem.at[0])
    finish_sends(0)
    finish_sends(1)


def write_out(a, b, c, a_out, b_out, c_out, sem):
    copies = [
        pltpu.make_async_copy(src, dst, sem.at[i])
        for i, (src, dst) in enumerate(((a, a_out), (b, b_out), (c, c_out)))
    ]
    for copy in copies:
        copy.start()
    for copy in copies:
        copy.wait()


def shards(queries, keys, values, out_grad, norm_gain):
    tokens, width = queries.shape
    vmem = pltpu.VMEM
    grad = jax.ShapeDtypeStruct((tokens, width), bf16)
    hbm = pl.BlockSpec(memory_space=pltpu.HBM)
    on_chip = pl.BlockSpec(memory_space=pltpu.VMEM)
    dma = pltpu.SemaphoreType.DMA
    flat = (2, CHUNKS, PER * DH, DH)
    by_y = (2, CHUNKS, NY, YROWS, DH)
    by_z = (2, CHUNKS, NZ, ZROWS, DH)
    pairs = (2, CHUNKS, 2)
    results = pl.pallas_call(
        kernel,
        out_shape=(grad, grad, grad),
        in_specs=[hbm, hbm, hbm, hbm, hbm],
        out_specs=(on_chip, on_chip, on_chip),
        scratch_shapes=[
            vmem((tokens, width), bf16),
            vmem((tokens, width), bf16),
            vmem((tokens, width), bf16),
            vmem((tokens, width), bf16),
            vmem((width,), bf16),
            vmem((HEADS, DH, GROUP), bf16),
            vmem((tokens, width), f32),
            vmem((tokens, width), f32),
            vmem((tokens, width), bf16),
            vmem((HEADS, GROUP, GROUP), bf16),
            vmem((HEADS, GROUP, GROUP), bf16),
            vmem((tokens, width), f32),
            vmem((tokens, width), f32),
            vmem((HEADS, DH, DH), bf16),
            vmem((2, 2, CHUNKS, PER * DH, DH), f32),
            vmem(flat, f32),
            vmem(by_y, f32),
            vmem(by_y, f32),
            vmem(by_z, f32),
            vmem(by_z, f32),
            vmem(by_z, f32),
            vmem(by_z, f32),
            vmem(by_y, f32),
            vmem(by_y, f32),
            vmem(flat, f32),
            vmem(flat, f32),
            vmem((2, GROUP, DH), f32),
            vmem((NX, 8, GROUP), f32),
            dma((5,)),
            dma(pairs),
            dma(pairs),
            dma(pairs),
            dma(pairs),
            dma(pairs),
            dma(pairs),
            dma((2,)),
        ],
        compiler_params=pltpu.CompilerParams(
            collective_id=0, has_side_effects=True, vmem_limit_bytes=46 * 2**20
        ),
        name="block_backward",
    )(
        *(
            pltpu.with_memory_space_constraint(arg, pltpu.HBM)
            for arg in (queries, keys, values, out_grad, norm_gain)
        )
    )
    return pl.pallas_call(
        write_out,
        out_shape=(grad, grad, grad),
        in_specs=[on_chip, on_chip, on_chip],
        out_specs=(hbm, hbm, hbm),
        scratch_shapes=[dma((3,))],
        compiler_params=pltpu.CompilerParams(vmem_limit_bytes=4 * 2**20),
        name="stage_out",
    )(*results)


def solution(mesh):
    return jax.shard_map(
        shards,
        mesh=mesh,
        in_specs=(
            P("seq", "head"),
            P("seq", "head"),
            P("seq", "head"),
            P("seq", "head"),
            P("head"),
        ),
        out_specs=(P("seq", "head"), P("seq", "head"), P("seq", "head")),
        check_vma=False,
    )
```

```python
import functools

import jax
import jax.numpy as jnp
from jax import lax
from jax.experimental import pallas as pl
from jax.experimental.pallas import tpu as pltpu
from jax.sharding import PartitionSpec as P

DH = 128
GROUP = 256
HEADS = 16
HALF = 8
NZ = 8
NY = 4
NX = 4
CHUNKS = 4
PER = HALF // CHUNKS
YROWS = PER * DH // NY
ZROWS = YROWS // NZ
MESH = pl.DeviceIdType.MESH
FAR_Z = (4, 3, 5, 2, 6, 1, 7)
FAR_Y = (2, 1, 3)
FIRST = (
    "y0", "y1", "y2", "y3", "w", "z0", "w", "z1", "w", "z2", "r0", "z3", "w", "r1", "w", "r2",
    "b0", "r3", "w", "b1", "b2", "b3", "c0", "c1", "t0", "c2", "t1", "c3", "t2", "t3",
)
SECOND = (
    "s0", "s1", "y0", "s2", "y1", "s3", "y2", "y3", "w", "z0", "w", "z1", "w", "z2", "r0", "z3",
    "w", "r1", "w", "r2", "b0", "r3", "w", "b1", "w", "b2", "b3", "w", "c0", "c1", "t0", "c2",
    "t1", "c3", "t2", "t3",
)
PEERS = 1 + len(FAR_Z) + len(FAR_Y) + NX - 1

f32 = jnp.float32
bf16 = jnp.bfloat16


def dot(a, b, dim_a, dim_b):
    return lax.dot_general(
        a, b, (((dim_a,), (dim_b,)), ((), ())), preferred_element_type=f32
    )


def wait_for(ref, sem):
    pltpu.make_async_copy(ref, ref, sem).wait()


def kernel(
    q_hbm, k_hbm, v_hbm, g_hbm, gain_hbm,
    qg, kg, vg,
    q, k, v, g, gain, q_t, attn, scaled, delta, scores, dscore, kg_part, vg_part, state,
    own, swap, chip, y_got, y_sum, z_got, z_part, z_back, y_part, y_back, ahead, arrived,
    norm_acc, norm_got,
    in_sem, swap_sem, y_sem, z_sem, zb_sem, yb_sem, ahead_sem, norm_sem,
):
    seq = lax.axis_index("seq")
    plane = lax.axis_index("head")
    core = lax.rem(seq, 2)
    z, y = seq // (2 * NY), lax.rem(seq // 2, NY)
    other = (seq + 1 - 2 * core, plane)
    y_peers = [lax.rem(y + step, NY) for step in FAR_Y]
    z_peers = [lax.rem(z + step, NZ) for step in FAR_Z]

    def at_y(place):
        return ((z * NY + place) * 2 + core, plane)

    def at_z(place):
        return ((place * NY + y) * 2 + core, plane)

    def across(step):
        return (seq, lax.rem(plane + step, NX))

    loads = [
        pltpu.make_async_copy(src, dst, in_sem.at[i])
        for i, (src, dst) in enumerate(
            ((k_hbm, k), (v_hbm, v), (q_hbm, q), (g_hbm, g), (gain_hbm, gain))
        )
    ]
    for load in loads[:2]:
        load.start()

    barrier = pltpu.get_barrier_semaphore()
    for place in z_peers:
        pl.semaphore_signal(barrier, inc=1, device_id=at_z(place), device_id_type=MESH)
    for place in y_peers:
        pl.semaphore_signal(barrier, inc=1, device_id=at_y(place), device_id_type=MESH)
    for step in range(1, NX):
        pl.semaphore_signal(barrier, inc=1, device_id=across(step), device_id_type=MESH)
    pl.semaphore_signal(barrier, inc=1, device_id=other, device_id_type=MESH)

    mine = core * HALF
    theirs = HALF - mine

    def cols(head):
        return pl.ds(pl.multiple_of(head * DH, DH), DH)

    def send(src, dst, sem, device):
        pltpu.make_async_remote_copy(
            src_ref=src,
            dst_ref=dst,
            send_sem=sem.at[0],
            recv_sem=sem.at[1],
            device_id=device,
            device_id_type=MESH,
        ).start()

    def fill(s, c, term):
        for j in range(PER):
            own[s, 1 - core, c, pl.ds(j * DH, DH)] = term(theirs + c * PER + j)

    def swap_out(s, c):
        send(own.at[s, 1 - core, c], swap.at[s, c], swap_sem.at[s, c], other)

    def y_out(s, c, term):
        for j in range(PER):
            own[s, core, c, pl.ds(j * DH, DH)] = term(mine + c * PER + j)
        wait_for(swap.at[s, c], swap_sem.at[s, c, 1])
        chip[s, c] = (own[s, core, c] + swap[s, c]).reshape(NY, YROWS, DH)
        for place in y_peers:
            send(chip.at[s, c, place], y_got.at[s, c, y], y_sem.at[s, c], at_y(place))
        y_got[s, c, y] = chip[s, c, y]

    def z_out(s, c):
        wait_for(y_got.at[s, c, pl.ds(0, NY - 1)], y_sem.at[s, c, 1])
        total = (y_got[s, c, 0] + y_got[s, c, 1]) + (y_got[s, c, 2] + y_got[s, c, 3])
        y_sum[s, c] = total.reshape(NZ, ZROWS, DH)
        for place in z_peers:
            send(y_sum.at[s, c, place], z_got.at[s, c, z], z_sem.at[s, c], at_z(place))
        z_got[s, c, z] = y_sum[s, c, z]

    def z_return(s, c, reverse):
        wait_for(z_got.at[s, c, pl.ds(0, NZ - 1)], z_sem.at[s, c, 1])
        total = jnp.zeros((ZROWS, DH), f32)
        for place in range(NZ - 1, -1, -1) if reverse else range(NZ):
            z_part[s, c, place] = total
            total = total + z_got[s, c, place]
        for place in z_peers:
            send(z_part.at[s, c, place], z_back.at[s, c, z], zb_sem.at[s, c], at_z(place))
        z_back[s, c, z] = z_part[s, c, z]

    def y_return(s, c, reverse):
        wait_for(z_back.at[s, c, pl.ds(0, NZ - 1)], zb_sem.at[s, c, 1])
        total = z_back[s, c].reshape(YROWS, DH)
        for place in range(NY - 1, -1, -1) if reverse else range(NY):
            y_part[s, c, place] = total
            total = total + y_got[s, c, place]
        for place in y_peers:
            send(y_part.at[s, c, place], y_back.at[s, c, y], yb_sem.at[s, c], at_y(place))
        y_back[s, c, y] = y_part[s, c, y]

    def collect(s, c, inner, use):
        wait_for(y_back.at[s, c, pl.ds(0, NY - 1)], yb_sem.at[s, c, 1])
        chip_part = y_back[s, c].reshape(PER * DH, DH)
        is_inner = core == inner
        both = chip_part + jnp.where(is_inner, own[s, core, c], swap[s, c])
        ahead[s, c] = jnp.where(is_inner, both, chip_part)
        send(ahead.at[s, c], arrived.at[s, c], ahead_sem.at[s, c], other)
        result = jnp.where(is_inner, chip_part, both).astype(bf16)
        for j in range(PER):
            use(mine + c * PER + j, result[j * DH:(j + 1) * DH])

    def collect_theirs(s, c, use):
        wait_for(arrived.at[s, c], ahead_sem.at[s, c, 1])
        result = arrived[s, c].astype(bf16)
        for j in range(PER):
            use(theirs + c * PER + j, result[j * DH:(j + 1) * DH])

    def finish_sends(s):
        for c in range(CHUNKS):
            wait_for(swap.at[s, c], swap_sem.at[s, c, 0])
            wait_for(y_got.at[s, c, pl.ds(0, NY - 1)], y_sem.at[s, c, 0])
            wait_for(z_got.at[s, c, pl.ds(0, NZ - 1)], z_sem.at[s, c, 0])
            wait_for(z_back.at[s, c, pl.ds(0, NZ - 1)], zb_sem.at[s, c, 0])
            wait_for(y_back.at[s, c, pl.ds(0, NY - 1)], yb_sem.at[s, c, 0])
            wait_for(arrived.at[s, c], ahead_sem.at[s, c, 0])

    def run(order, s, reverse, term, inner, use, local):
        local = list(local)
        for step in order:
            name, c = step[0], int(step[1:] or 0)
            if name == "s":
                fill(s, c, term)
                swap_out(s, c)
            elif name == "y":
                y_out(s, c, term)
            elif name == "z":
                z_out(s, c)
            elif name == "r":
                z_return(s, c, reverse)
            elif name == "b":
                y_return(s, c, reverse)
            elif name == "c":
                collect(s, c, inner, use)
            elif name == "t":
                collect_theirs(s, c, use)
            else:
                local.pop(0)()
        assert not local

    def heads(first, count, body):
        def pair(i, carry):
            body(first + 2 * i)
            body(first + 2 * i + 1)
            return carry

        lax.fori_loop(0, count // 2, pair, 0)

    chunks = range(CHUNKS)
    rows = lax.broadcasted_iota(jnp.int32, (GROUP, GROUP), 0)
    columns = lax.broadcasted_iota(jnp.int32, (GROUP, GROUP), 1)
    causal = rows >= columns

    def key_value(head):
        return dot(k[:, cols(head)], v[:, cols(head)], 0, 0)

    loads[0].wait()
    loads[1].wait()
    for c in chunks:
        fill(0, c, key_value)
    for load in loads[2:]:
        load.start()
    pl.semaphore_wait(barrier, PEERS)
    for c in chunks:
        swap_out(0, c)

    def within(head):
        at = cols(head)
        part = dot(q[:, at], k[:, at], 1, 1)
        masked = jnp.where(causal, part, 0.0).astype(bf16)
        scores[head] = masked
        attn[:, at] = dot(masked, v[:, at], 1, 0)

    def prepare(i, carry):
        for head in (2 * i, 2 * i + 1):
            q_t[head] = q[:, cols(head)].T
        at = pl.ds(pl.multiple_of(i * 2 * DH, 2 * DH), 2 * DH)
        scaled[:, at] = gain[at].astype(f32).reshape(1, 2 * DH) * g[:, at].astype(f32)
        return carry

    norm_acc[...] = jnp.zeros_like(norm_acc)

    def finish_attn(head, state_b):
        at = cols(head)
        state[head] = state_b
        value = attn[:, at] + dot(q[:, at], state_b, 1, 0)
        attn[:, at] = value
        norm_acc[0] += value * value
        norm_acc[1] += scaled[:, at] * value

    def load_rest():
        for load in loads[2:]:
            load.wait()

    run(
        FIRST, 0, False, key_value, 0, finish_attn,
        [load_rest]
        + [functools.partial(heads, i, 4, within) for i in range(0, HEADS, 4)]
        + [lambda: lax.fori_loop(0, HEADS // 2, prepare, 0)],
    )

    norm_got[plane, 0:1] = jnp.sum(norm_acc[0].T, axis=0, keepdims=True)
    norm_got[plane, 1:2] = jnp.sum(norm_acc[1].T, axis=0, keepdims=True)
    for step in (2, 1, 3):
        send(norm_got.at[plane], norm_got.at[plane], norm_sem, across(step))
    wait_for(norm_got.at[pl.ds(0, NX - 1)], norm_sem.at[1])
    sums = (norm_got[0] + norm_got[1]) + (norm_got[2] + norm_got[3])
    features = float(NX * HEADS * DH)
    inverse = lax.rsqrt(sums[0:1] / features + 1e-05)
    weight = inverse * inverse * inverse * (sums[1:2] / features)
    norm_acc[0] = jnp.broadcast_to(inverse, (DH, GROUP)).T
    norm_acc[1] = jnp.broadcast_to(weight, (DH, GROUP)).T

    def query_delta(head):
        at = cols(head)
        value = (norm_acc[0] * scaled[:, at] - attn[:, at] * norm_acc[1]).astype(bf16)
        delta[:, at] = value
        return dot(q_t[head], value, 1, 0)

    def query_side(head):
        at = cols(head)
        part = dot(delta[:, at], v[:, at], 1, 1)
        masked = jnp.where(causal, part, 0.0).astype(bf16)
        dscore[head] = masked
        grad = dot(masked, k[:, at], 1, 0) + dot(delta[:, at], state[head], 1, 1)
        qg[:, at] = grad.astype(bf16)

    def key_side(head):
        at = cols(head)
        kg_part[:, at] = dot(dscore[head], q[:, at], 0, 0)
        vg_part[:, at] = dot(scores[head], delta[:, at], 0, 0)

    def finish_keys(head, later_b):
        at = cols(head)
        kg[:, at] = (kg_part[:, at] + dot(v[:, at], later_b, 1, 1)).astype(bf16)
        vg[:, at] = (vg_part[:, at] + dot(k[:, at], later_b, 1, 0)).astype(bf16)

    run(
        SECOND, 1, True, query_delta, 1, finish_keys,
        [functools.partial(heads, i, 4, query_side) for i in range(0, HEADS, 4)]
        + [functools.partial(heads, i, 4, key_side) for i in range(0, HEADS, 4)],
    )
    wait_for(norm_got.at[pl.ds(0, NX - 1)], norm_sem.at[0])
    finish_sends(0)
    finish_sends(1)


def write_out(a, b, c, a_out, b_out, c_out, sem):
    copies = [
        pltpu.make_async_copy(src, dst, sem.at[i])
        for i, (src, dst) in enumerate(((a, a_out), (b, b_out), (c, c_out)))
    ]
    for copy in copies:
        copy.start()
    for copy in copies:
        copy.wait()


def shards(queries, keys, values, out_grad, norm_gain):
    tokens, width = queries.shape
    vmem = pltpu.VMEM
    grad = jax.ShapeDtypeStruct((tokens, width), bf16)
    hbm = pl.BlockSpec(memory_space=pltpu.HBM)
    on_chip = pl.BlockSpec(memory_space=pltpu.VMEM)
    dma = pltpu.SemaphoreType.DMA
    flat = (2, CHUNKS, PER * DH, DH)
    by_y = (2, CHUNKS, NY, YROWS, DH)
    by_z = (2, CHUNKS, NZ, ZROWS, DH)
    pairs = (2, CHUNKS, 2)
    results = pl.pallas_call(
        kernel,
        out_shape=(grad, grad, grad),
        in_specs=[hbm, hbm, hbm, hbm, hbm],
        out_specs=(on_chip, on_chip, on_chip),
        scratch_shapes=[
            vmem((tokens, width), bf16),
            vmem((tokens, width), bf16),
            vmem((tokens, width), bf16),
            vmem((tokens, width), bf16),
            vmem((width,), bf16),
            vmem((HEADS, DH, GROUP), bf16),
            vmem((tokens, width), f32),
            vmem((tokens, width), f32),
            vmem((tokens, width), bf16),
            vmem((HEADS, GROUP, GROUP), bf16),
            vmem((HEADS, GROUP, GROUP), bf16),
            vmem((tokens, width), f32),
            vmem((tokens, width), f32),
            vmem((HEADS, DH, DH), bf16),
            vmem((2, 2, CHUNKS, PER * DH, DH), f32),
            vmem(flat, f32),
            vmem(by_y, f32),
            vmem(by_y, f32),
            vmem(by_z, f32),
            vmem(by_z, f32),
            vmem(by_z, f32),
            vmem(by_z, f32),
            vmem(by_y, f32),
            vmem(by_y, f32),
            vmem(flat, f32),
            vmem(flat, f32),
            vmem((2, GROUP, DH), f32),
            vmem((NX, 8, GROUP), f32),
            dma((5,)),
            dma(pairs),
            dma(pairs),
            dma(pairs),
            dma(pairs),
            dma(pairs),
            dma(pairs),
            dma((2,)),
        ],
        compiler_params=pltpu.CompilerParams(
            collective_id=0, has_side_effects=True, vmem_limit_bytes=46 * 2**20
        ),
        name="block_backward",
    )(
        *(
            pltpu.with_memory_space_constraint(arg, pltpu.HBM)
            for arg in (queries, keys, values, out_grad, norm_gain)
        )
    )
    return pl.pallas_call(
        write_out,
        out_shape=(grad, grad, grad),
        in_specs=[on_chip, on_chip, on_chip],
        out_specs=(hbm, hbm, hbm),
        scratch_shapes=[dma((3,))],
        compiler_params=pltpu.CompilerParams(vmem_limit_bytes=4 * 2**20),
        name="stage_out",
    )(*results)


def solution(mesh):
    return jax.shard_map(
        shards,
        mesh=mesh,
        in_specs=(
            P("seq", "head"),
            P("seq", "head"),
            P("seq", "head"),
            P("seq", "head"),
            P("head"),
        ),
        out_specs=(P("seq", "head"), P("seq", "head"), P("seq", "head")),
        check_vma=False,
    )
```
